32 devices in a mesh: dp: 4 (over x, core), tensor: 8 (over z, y).
Axes of the slice: x: 2, y: 2, z: 4, core: 2. Of those that a mesh axis runs over, the one named last changes fastest.
Arguments:
- queries: bfloat16 [2048, 8192], P('dp', 'tensor'), may hold values from -60 to 60
- keys_values: bfloat16 [2, 2048, 1024], P(None, 'dp'), may hold values from -7 to 7
- out_weight: bfloat16 [8192, 8192], P('tensor'), may hold values from -0.0625 to 0.0625
- cotangent: bfloat16 [2048, 8192], P(('dp', 'tensor')), may hold values from -6 to 6
- head_pick: int32 [12, 64], replicated, may hold values from 0 to 1, as said below
- owner_index: int32 [12, 1], replicated, may hold values from 0 to 3; in each aligned block of 12 rows (0 to 11, 12 to 23, ...) at most 3 rows name the same one
Outputs:
- query_grad: bfloat16 [2048, 8192], P('dp', 'tensor')
- weight_grad: float32 [12, 128, 8192], P('dp', None, 'tensor')
The draws below stay inside these ranges and needn't reach their ends.
Inputs may be any that keep to these rules, and one draw needn't show every extreme that they name: `head_pick`: each row has a single 1; no head is named twice. `owner_index`: no data index owns more than 3 selected heads, and one owns exactly 3.
All inputs are finite; a program needn't handle non-finite values.
Results may differ from the reference program's by a relative error of at most 0.008.
Values may be sent and summed in bfloat16 or wider, within the bound.
A program may use at most 192 MiB of HBM per device.

```python
import math
import jax
import jax.numpy as jnp
import numpy as np
from jax import lax

D = 8192
H = 64
HD = 128
KVH = 8
SEL = 12
CAP = 3
TOKENS_GROUP = 512
TOKENS = 2048
N_DP = 4


def shared_keys(key):
    shape = (TOKENS, KVH * HD)
    return jnp.clip(jax.random.normal(jax.random.fold_in(key, 11), shape, jnp.float32), -6.0, 6.0)


def draw_keys_values(key, part):
    keys_part = shared_keys(key)
    shape = (TOKENS, KVH * HD)
    values_part = jnp.clip(jax.random.normal(jax.random.fold_in(key, 13), shape, jnp.float32), -6.0, 6.0)
    return jnp.stack([keys_part, values_part]).astype(jnp.bfloat16)


def draw_queries(key, part):
    shape = (TOKENS, H * HD)
    result = jnp.clip(jax.random.normal(jax.random.fold_in(key, 21), shape, jnp.float32), -6.0, 6.0)
    return result.astype(jnp.bfloat16)


def draw_head_pick(key, part):
    chosen = jax.random.permutation(jax.random.fold_in(key, 31), H)[:SEL]
    return (chosen[:, None] == jnp.arange(H)[None, :]).astype(jnp.int32)


def levels(key, extent, split, smallest, high):
    loudness, own = 1.0, jax.random.fold_in(key, 6)
    for dim, parts in split:
        draws = jnp.exp(jax.random.uniform(jax.random.fold_in(own, dim), (parts,), jnp.float32, smallest / len(split), high / len(split)))
        loudness = loudness * jnp.repeat(draws, extent[dim] // parts).reshape([-1 if axis == dim else 1 for axis in range(len(extent))])
    return loudness


def shared_out(own_key, own, number, rows, count, top, reach, lean):
    order = jax.random.permutation(own_key, count)
    heavy_load, usual = portions_of(count, rows * top, reach, lean, True), portions_of(count, rows * top, reach, lean, False)
    places = jnp.arange(count)

    def named(tallies, rotation):
        used = int((tallies > 0).sum())
        fixed = max(1, used // 4)
        passed = fixed + (places - fixed + rotation * (used - fixed)) % max(1, count - fixed)
        return jnp.zeros((count,), jnp.int32).at[order[jnp.where(places < fixed, places, passed)]].set(jnp.asarray(tallies, jnp.int32))

    tallies = jnp.where(number % 4 == 0, named(heavy_load, number // 4), named(usual, number - number // 4 - 1))
    mixed = jax.random.permutation(jax.random.fold_in(own, 3), count)
    donor, receiver = mixed[0:count // 2 * 2:2], mixed[1:count // 2 * 2:2]
    slack = jnp.minimum(tallies[donor] - 1, reach - tallies[receiver]) // 2
    slack = jnp.where((donor == order[0]) | (receiver == order[0]) | (tallies[receiver] == 0), 0, jnp.maximum(slack, 0))
    passed = jax.random.randint(jax.random.fold_in(own, 4), (count // 2,), 0, 1 << 20) % (slack + 1)
    tallies = tallies.at[donor].add(-passed).at[receiver].add(passed)
    members = jnp.searchsorted(jnp.cumsum(tallies), jnp.arange(rows * top), side="right").astype(jnp.int32)
    table = members.reshape(top, rows).T
    table = table[jax.random.permutation(jax.random.fold_in(own, 1), rows)]
    rotation = jax.random.randint(jax.random.fold_in(own, 2), (rows, 1), 0, top)
    return jnp.take_along_axis(table, (jnp.arange(top)[None, :] + rotation) % top, axis=1)


def portions_of(number_of, total, limit, skew, full):
    loads = [(1 << 20) // math.isqrt(standing ** skew) + 1 for standing in range(1, number_of + 1)]
    largest = limit if full else min(limit, max(-(-total // number_of), total * loads[0] // sum(loads)))
    least = 1 if total - largest >= number_of - 1 else 0
    counts, spare = [largest] + [least] * (number_of - 1), total - largest - least * (number_of - 1)
    while spare > 0:
        movable = [i for i in range(1, number_of) if counts[i] < largest] or [i for i in range(1, number_of) if counts[i] < limit]
        whole, left = sum([loads[i] for i in movable]), spare
        for i in movable:
            addition = min(limit - counts[i], max(1, left * loads[i] // whole), spare)
            counts[i] = counts[i] + addition
            spare = spare - addition
    return np.array(counts)


def bell_draw(own_key, extent, scale, most, cuts=(), kind=jnp.bfloat16):
    gain = levels(own_key, extent, cuts, -0.22, 0.18) if cuts else 1.0
    drawn = jax.random.normal(own_key, extent, jnp.float32) * scale * gain
    return jnp.minimum(jnp.maximum(drawn, -most), most).astype(kind)


def setup_inputs(seed: int = 0) -> dict:
    key_list = jax.random.split(jax.random.key(seed), 7)
    queries = draw_queries(jax.random.fold_in(key_list[6], 71), 0)
    keys_values = draw_keys_values(jax.random.fold_in(key_list[6], 71), 0)
    out_weight = bell_draw(key_list[2], (H * HD, D), (H * HD) ** -0.5, 0.0625, ((0, 8),))
    cotangent = bell_draw(key_list[3], (TOKENS, D), 1.0, 6.0, ((0, 32),))
    head_pick = draw_head_pick(jax.random.fold_in(key_list[6], 71), 0)
    owner_index_keys = jax.random.split(jax.random.fold_in(key_list[5], 1), SEL // SEL)
    owner_index_turns = jax.random.permutation(jax.random.fold_in(key_list[5], 3), SEL // SEL)
    owner_index = jax.vmap(lambda own, number: shared_out(jax.random.fold_in(key_list[5], 2), own, number, SEL, N_DP, 1, CAP, 2))(owner_index_keys, owner_index_turns).reshape((SEL, 1))
    return dict(queries=queries, keys_values=keys_values, out_weight=out_weight, cotangent=cotangent, head_pick=head_pick, owner_index=owner_index)


def route_table(owner_index, groups, capacity):
    chosen = owner_index[:, 0]
    picked_count = chosen.shape[0]
    matches = (chosen[:, None] == chosen[None, :]).astype(jnp.int32)
    order = jnp.arange(picked_count, dtype=jnp.int32)
    earlier = (order[:, None] > order[None, :]).astype(jnp.int32)
    slot_index = lax.optimization_barrier(jnp.sum(matches * earlier, axis=1))
    target = chosen * capacity + slot_index
    places = jnp.arange(groups * capacity, dtype=jnp.int32)
    return (places[:, None] == target[None, :]).astype(jnp.float32)

def reference(queries, keys_values, out_weight, cotangent, head_pick, owner_index):
    score_scale = 1.0 / math.sqrt(HD)
    group_rows = TOKENS_GROUP
    positions = jnp.arange(group_rows, dtype=jnp.int32)
    allowed = positions[:, None] >= positions[None, :]

    def one_group(total, group_index):
        start = (group_index * group_rows).astype(jnp.int32)
        query_rows = lax.dynamic_slice_in_dim(queries, start, group_rows, 0)
        kv_rows = lax.dynamic_slice_in_dim(keys_values, start, group_rows, 1)
        grad_rows = lax.dynamic_slice_in_dim(cotangent, start, group_rows, 0)
        input_grad = jnp.dot(grad_rows, out_weight.T, preferred_element_type=jnp.float32).astype(jnp.bfloat16)

        def one_head(head_index):
            kv_head = (head_index // (H // KVH)).astype(jnp.int32)
            query_head = lax.dynamic_slice_in_dim(query_rows, head_index * HD, HD, 1)
            key_head = lax.dynamic_slice_in_dim(kv_rows[0], kv_head * HD, HD, 1)
            value_head = lax.dynamic_slice_in_dim(kv_rows[1], kv_head * HD, HD, 1)
            grad_head = lax.dynamic_slice_in_dim(input_grad, head_index * HD, HD, 1)
            scores = jnp.dot(query_head, key_head.T, preferred_element_type=jnp.float32) * score_scale
            scores = jnp.where(allowed, scores, -jnp.inf)
            peak = lax.optimization_barrier(jnp.max(scores, axis=1, keepdims=True))
            weights = jnp.exp(scores - peak)
            probs = weights / lax.optimization_barrier(jnp.sum(weights, axis=1, keepdims=True))
            attended = jnp.dot(probs.astype(jnp.bfloat16), value_head, preferred_element_type=jnp.float32).astype(jnp.bfloat16)
            prob_grad = jnp.dot(grad_head, value_head.T, preferred_element_type=jnp.float32)
            row_delta = lax.optimization_barrier(jnp.sum(grad_head.astype(jnp.float32) * attended.astype(jnp.float32), axis=1))
            score_grad = (probs * (prob_grad - row_delta[:, None])).astype(jnp.bfloat16)
            query_grad = (jnp.dot(score_grad, key_head, preferred_element_type=jnp.float32) * score_scale).astype(jnp.bfloat16)
            return (attended, query_grad)
        attended, query_grad = lax.map(one_head, jnp.arange(H, dtype=jnp.int32))
        picked = jnp.einsum('sh,htd->tsd', head_pick.astype(jnp.float32), attended.astype(jnp.float32), precision=lax.Precision.HIGHEST)
        partial_value = jnp.einsum('tsd,tc->sdc', picked, grad_rows.astype(jnp.float32), precision=lax.Precision.HIGHEST)
        return (total + partial_value, query_grad)
    initial = jnp.zeros((SEL, HD, D), jnp.float32)
    head_grad, query_grad = lax.scan(one_group, initial, jnp.arange(N_DP, dtype=jnp.int32))
    query_grad = jnp.transpose(query_grad, (0, 2, 1, 3)).reshape(TOKENS, H * HD)
    routing = route_table(owner_index, N_DP, CAP)
    weight_grad = jnp.einsum('ps,sdc->pdc', routing, head_grad, precision=lax.Precision.HIGHEST)
    return (query_grad, weight_grad)
```

```python
import functools
import math

import jax
import jax.numpy as jnp
from jax import lax
from jax.experimental import pallas as pl
from jax.experimental.pallas import tpu as pltpu
from jax.sharding import PartitionSpec as P

H = 64
HD = 128
KVH = 8
CAP = 3
MESH = pl.DeviceIdType.MESH


def route_table(owner_index, groups, capacity):
    chosen = owner_index[:, 0]
    picked_count = chosen.shape[0]
    matches = (chosen[:, None] == chosen[None, :]).astype(jnp.int32)
    order = jnp.arange(picked_count, dtype=jnp.int32)
    earlier = (order[:, None] > order[None, :]).astype(jnp.int32)
    slot_index = jnp.sum(matches * earlier, axis=1)
    target = chosen * capacity + slot_index
    places = jnp.arange(groups * capacity, dtype=jnp.int32)
    return (places[:, None] == target[None, :]).astype(jnp.float32)


def ring_member(place, n):
    late = place // (n // 2)
    return (1 - late) * (2 * place) + late * (2 * (n - 1 - place) + 1)


def ring_place(index, n):
    odd = index % 2
    return (1 - odd) * (index // 2) + odd * (n - 1 - index // 2)


def slot_of(direction, hop, n):
    if hop == 0:
        return 0
    if hop == n // 2:
        return n - 1
    return 2 * hop - 1 + direction


def gather_kernel(n, cot_ref, w_ref, ig_ref, slab_ref, held, wbuf, acc, send_sem, recv_sem, local_sem):
    rows, width = cot_ref.shape
    half = width // 2
    last = n // 2
    me = lax.axis_index("tensor")
    place = ring_place(me, n)
    to = (ring_member((place + 1) % n, n), ring_member((place + n - 1) % n, n))

    w_copy = pltpu.make_async_copy(w_ref, wbuf, local_sem.at[0])
    w_copy.start()
    own_copy = pltpu.make_async_copy(cot_ref, held.at[0], local_sem.at[1])
    own_copy.start()

    barrier = pltpu.get_barrier_semaphore()
    for target in to:
        pl.semaphore_signal(barrier, inc=1, device_id={"tensor": target}, device_id_type=MESH)
    pl.semaphore_wait(barrier, 2)

    def send(direction, hop, part):
        columns = pl.ds(part * half, half)
        source = cot_ref if hop == 1 else held.at[slot_of(direction, hop - 1, n)]
        return pltpu.make_async_remote_copy(
            src_ref=source.at[:, columns],
            dst_ref=held.at[slot_of(direction, hop, n), :, columns],
            send_sem=send_sem.at[direction, hop - 1, part],
            recv_sem=recv_sem.at[direction, hop - 1, part],
            device_id={"tensor": to[direction]},
            device_id_type=MESH,
        )

    def parts(direction, hop):
        order = (0, 1) if direction == 0 else (1, 0)
        return order if hop < last else order[:1]

    sent = {}
    for turn in range(2):
        for direction in range(2):
            part = parts(direction, 1)[turn]
            sent[direction, 1, part] = send(direction, 1, part)
            sent[direction, 1, part].start()

    own_copy.wait()
    w_copy.wait()
    step = 1024
    my_columns = pl.ds(pl.multiple_of(me * (width // n), width // n), width // n)

    def product(first, count):
        acc[...] = jnp.zeros_like(acc)

        def body(k, carry):
            columns = pl.ds(pl.multiple_of(k * step, step), step)
            block = held[first : first + count, :, columns].reshape(count * rows, step)
            acc[: count * rows, :] += lax.dot_general(
                block,
                wbuf[:, columns],
                (((1,), (1,)), ((), ())),
                preferred_element_type=jnp.float32,
            )
            return carry

        lax.fori_loop(0, width // step, body, 0)

    def store(slot, at, origin):
        target = pl.ds(pl.multiple_of(origin * rows, rows), rows)
        ig_ref[target, :] = acc[at * rows : (at + 1) * rows, :].astype(ig_ref.dtype)
        slab_ref[target, :] = held[slot, :, my_columns]

    product(0, 1)
    store(0, 0, me)
    for hop in range(1, last + 1):
        turns = 2 if hop < last else 1
        for turn in range(turns):
            for direction in range(2):
                part = parts(direction, hop)[turn]
                sent[direction, hop, part].wait_recv()
                if hop < last and part in parts(direction, hop + 1):
                    sent[direction, hop + 1, part] = send(direction, hop + 1, part)
                    sent[direction, hop + 1, part].start()
        first = slot_of(0, hop, n)
        product(first, turns)
        for direction in range(turns):
            shift = n - hop if direction == 0 else hop
            store(first + direction, direction, ring_member((place + shift) % n, n))
    for copy in sent.values():
        copy.wait_send()


def gather_and_multiply(cotangent, out_weight, n):
    rows, width = cotangent.shape
    outs = out_weight.shape[0]
    return pl.pallas_call(
        functools.partial(gather_kernel, n),
        out_shape=(
            jax.ShapeDtypeStruct((n * rows, outs), jnp.bfloat16),
            jax.ShapeDtypeStruct((n * rows, width // n), jnp.bfloat16),
        ),
        in_specs=[pl.BlockSpec(memory_space=pl.ANY)] * 2,
        out_specs=(pl.BlockSpec(memory_space=pltpu.VMEM),) * 2,
        scratch_shapes=[
            pltpu.VMEM((n, rows, width), jnp.bfloat16),
            pltpu.VMEM((outs, width), jnp.bfloat16),
            pltpu.VMEM((2 * rows, outs), jnp.float32),
            pltpu.SemaphoreType.DMA((2, n // 2, 2)),
            pltpu.SemaphoreType.DMA((2, n // 2, 2)),
            pltpu.SemaphoreType.DMA((2,)),
        ],
        compiler_params=pltpu.CompilerParams(
            collective_id=0, has_side_effects=True, vmem_limit_bytes=48 * 1024 * 1024
        ),
        cost_estimate=pl.CostEstimate(
            flops=2 * n * rows * width * outs,
            bytes_accessed=2 * width * (outs + 16 * n * rows),
            transcendentals=0,
        ),
    )(cotangent, out_weight)


def on_device(queries, keys_values, out_weight, cotangent, head_pick, owner_index):
    tensor_size = lax.axis_size("tensor")
    tensor_rank = lax.axis_index("tensor")
    group_rows = queries.shape[0]
    local_heads = queries.shape[1] // HD
    kv_head = tensor_rank * local_heads // (H // KVH)
    kv_local = lax.dynamic_slice_in_dim(keys_values, kv_head * HD, HD, 2)
    key_block = kv_local[0]
    value_block = kv_local[1]
    score_scale = 1.0 / math.sqrt(HD)
    query_heads = queries.reshape(group_rows, local_heads, HD)
    scores = (
        jnp.einsum("thd,sd->hts", query_heads, key_block, preferred_element_type=jnp.float32)
        * score_scale
    )
    positions = jnp.arange(group_rows, dtype=jnp.int32)
    allowed = positions[:, None] >= positions[None, :]
    scores = jnp.where(allowed[None], scores, -jnp.inf)
    peak = jnp.max(scores, axis=2, keepdims=True)
    weights = jnp.exp(scores - peak)
    probs = weights / jnp.sum(weights, axis=2, keepdims=True)
    attended = jnp.einsum(
        "hts,sd->thd", probs.astype(jnp.bfloat16), value_block, preferred_element_type=jnp.float32
    ).astype(jnp.bfloat16)

    routing = route_table(owner_index, lax.axis_size("dp"), CAP)
    places = routing.shape[0]
    local_pick = lax.dynamic_slice_in_dim(head_pick, tensor_rank * local_heads, local_heads, 1)
    wanted = jnp.sum(routing[:, :, None] * local_pick.astype(jnp.float32)[None], axis=1)
    chooser = (
        wanted.T.astype(jnp.bfloat16)[:, None, :, None]
        * jnp.eye(HD, dtype=jnp.bfloat16)[None, :, None, :]
    ).reshape(local_heads * HD, places * HD)
    mine = jnp.dot(
        attended.reshape(group_rows, local_heads * HD), chooser, preferred_element_type=jnp.float32
    ).astype(jnp.bfloat16)
    picked = lax.psum(mine, "tensor")

    input_grad, column_slab = gather_and_multiply(cotangent, out_weight, tensor_size)

    selected = lax.dot_general(
        picked, column_slab, (((0,), (0,)), ((), ())), preferred_element_type=jnp.float32
    ).astype(jnp.bfloat16)
    owned = lax.psum_scatter(selected, "dp", scatter_dimension=0, tiled=True)
    owned = owned.astype(jnp.float32).reshape(CAP, HD, -1)

    input_grad = input_grad.reshape(group_rows, local_heads, HD)
    prob_grad = jnp.einsum(
        "thd,sd->hts", input_grad, value_block, preferred_element_type=jnp.float32
    )
    row_delta = jnp.transpose(
        jnp.sum(input_grad.astype(jnp.float32) * attended.astype(jnp.float32), axis=2)
    )
    score_grad = (probs * (prob_grad - row_delta[:, :, None])).astype(jnp.bfloat16)
    query_grad = (
        jnp.einsum("hts,sd->thd", score_grad, key_block, preferred_element_type=jnp.float32)
        * score_scale
    )
    query_grad = query_grad.astype(jnp.bfloat16).reshape(group_rows, local_heads * HD)
    return (query_grad, owned)


def solution(mesh):
    placed = (
        P("dp", "tensor"),
        P(None, "dp", None),
        P("tensor", None),
        P(("dp", "tensor"), None),
        P(),
        P(),
    )
    return jax.shard_map(
        on_device,
        mesh=mesh,
        in_specs=placed,
        out_specs=(P("dp", "tensor"), P("dp", None, "tensor")),
        check_vma=False,
    )
```

```python
import functools
import math

import jax
import jax.numpy as jnp
from jax import lax
from jax.experimental import pallas as pl
from jax.experimental.pallas import tpu as pltpu
from jax.sharding import PartitionSpec as P

H = 64
HD = 128
KVH = 8
CAP = 3
MESH = pl.DeviceIdType.MESH


def route_table(owner_index, groups, capacity):
    chosen = owner_index[:, 0]
    picked_count = chosen.shape[0]
    matches = (chosen[:, None] == chosen[None, :]).astype(jnp.int32)
    order = jnp.arange(picked_count, dtype=jnp.int32)
    earlier = (order[:, None] > order[None, :]).astype(jnp.int32)
    slot_index = jnp.sum(matches * earlier, axis=1)
    target = chosen * capacity + slot_index
    places = jnp.arange(groups * capacity, dtype=jnp.int32)
    return (places[:, None] == target[None, :]).astype(jnp.float32)


def ring_member(place, n):
    late = place // (n // 2)
    return (1 - late) * (2 * place) + late * (2 * (n - 1 - place) + 1)


def ring_place(index, n):
    odd = index % 2
    return (1 - odd) * (index // 2) + odd * (n - 1 - index // 2)


def slot_of(direction, hop, n):
    if hop == 0:
        return 0
    if hop == n // 2:
        return n - 1
    return 2 * hop - 1 + direction


def block_kernel(
    n, cot_ref, w_ref, q_ref, kv_ref, chooser_ref,
    grad_ref, slab_ref, picked_ref,
    held, wbuf, acc, probs, attended, mine, sums,
    send_sem, recv_sem, sum_send, sum_recv, pick_send, pick_recv, local_sem,
):
    rows, width = cot_ref.shape
    half = width // 2
    last = n // 2
    tokens = n * rows
    heads = q_ref.shape[1] // HD
    lanes = mine.shape[1] // 2
    scale = 1.0 / math.sqrt(HD)
    me = lax.axis_index("tensor")
    place = ring_place(me, n)
    to = (ring_member((place + 1) % n, n), ring_member((place + n - 1) % n, n))

    w_copy = pltpu.make_async_copy(w_ref, wbuf, local_sem.at[0])
    w_copy.start()
    own_copy = pltpu.make_async_copy(cot_ref, held.at[0], local_sem.at[1])
    own_copy.start()

    barrier = pltpu.get_barrier_semaphore()
    for target in to:
        pl.semaphore_signal(barrier, inc=1, device_id={"tensor": target}, device_id_type=MESH)
    pl.semaphore_wait(barrier, 2)

    def remote(source, target, send, recv, direction):
        copy = pltpu.make_async_remote_copy(
            src_ref=source,
            dst_ref=target,
            send_sem=send,
            recv_sem=recv,
            device_id={"tensor": to[direction]},
            device_id_type=MESH,
        )
        copy.start()
        return copy

    def send_part(direction, hop, part):
        columns = pl.ds(part * half, half)
        source = cot_ref if hop == 1 else held.at[slot_of(direction, hop - 1, n)]
        return remote(
            source.at[:, columns],
            held.at[slot_of(direction, hop, n), :, columns],
            send_sem.at[direction, hop - 1, part],
            recv_sem.at[direction, hop - 1, part],
            direction,
        )

    def shard_rows(at):
        return pl.ds(pl.multiple_of(ring_member(at, n) * rows, rows), rows)

    def arrival(direction, hop):
        return (place + (n - hop if direction == 0 else hop)) % n

    def side(direction):
        return pl.ds(direction * lanes, lanes)

    def send_sum(direction, step):
        if step == 1:
            source = mine.at[shard_rows(arrival(direction, 1)), side(direction)]
        else:
            source = sums.at[direction, step - 2]
        return remote(
            source,
            sums.at[direction, step - 1],
            sum_send.at[direction, step - 1],
            sum_recv.at[direction, step - 1],
            direction,
        )

    def send_pick(direction, hop):
        columns = pl.ds(0, 2 * lanes) if hop < last else side(direction)
        return remote(
            picked_ref.at[slot_of(direction, hop - 1, n), :, columns],
            picked_ref.at[slot_of(direction, hop, n), :, columns],
            pick_send.at[direction, hop - 1],
            pick_recv.at[direction, hop - 1],
            direction,
        )

    sent, summed, picks = {}, {}, {}

    def sum_step(step):
        for direction in range(2):
            summed[direction, step].wait_recv()
            term = mine[shard_rows(arrival(direction, step + 1)), side(direction)]
            total = sums[direction, step - 1].astype(jnp.float32) + term.astype(jnp.float32)
            if step < n - 1:
                sums[direction, step - 1] = total.astype(jnp.bfloat16)
                summed[direction, step + 1] = send_sum(direction, step + 1)
            else:
                picked_ref[0, :, side(direction)] = total.astype(jnp.bfloat16)
        if step == n - 1:
            for direction in range(2):
                picks[direction, 1] = send_pick(direction, 1)

    def pick_step(hop):
        for direction in range(2):
            picks[direction, hop].wait_recv()
            if hop < last:
                picks[direction, hop + 1] = send_pick(direction, hop + 1)

    small = [functools.partial(sum_step, step) for step in range(1, n)]
    small += [functools.partial(pick_step, hop) for hop in range(1, last + 1)]

    def advance():
        if small:
            small.pop(0)()

    def parts(direction, hop):
        order = (0, 1) if direction == 0 else (1, 0)
        return order if hop < last else order[:1]

    for turn in range(2):
        for direction in range(2):
            part = parts(direction, 1)[turn]
            sent[direction, 1, part] = send_part(direction, 1, part)

    tile = 128

    def forward(head, carry):
        columns = pl.ds(pl.multiple_of(head * HD, HD), HD)
        for base in range(0, tokens, tile):
            span = base + tile
            score = (
                lax.dot_general(
                    q_ref[base:span, columns],
                    kv_ref[0, :span, :],
                    (((1,), (1,)), ((), ())),
                    preferred_element_type=jnp.float32,
                )
                * scale
            )
            at = lax.broadcasted_iota(jnp.int32, (tile, span), 0) + base
            key_at = lax.broadcasted_iota(jnp.int32, (tile, span), 1)
            score = jnp.where(at >= key_at, score, -jnp.inf)
            weight = jnp.exp(score - jnp.max(score, axis=1, keepdims=True))
            prob = (weight / jnp.sum(weight, axis=1, keepdims=True)).astype(jnp.bfloat16)
            probs[head, base:span, :span] = prob
            if span < tokens:
                probs[head, base:span, span:] = jnp.zeros((tile, tokens - span), jnp.bfloat16)
            attended[base:span, columns] = jnp.dot(
                prob, kv_ref[1, :span, :], preferred_element_type=jnp.float32
            ).astype(jnp.bfloat16)
        return carry

    lax.fori_loop(0, heads, forward, 0)

    def choose(block, carry):
        at = pl.ds(pl.multiple_of(block * tile, tile), tile)
        mine[at, :] = jnp.dot(
            attended[at, :], chooser_ref[...], preferred_element_type=jnp.float32
        ).astype(jnp.bfloat16)
        return carry

    lax.fori_loop(0, tokens // tile, choose, 0)
    for direction in range(2):
        summed[direction, 1] = send_sum(direction, 1)

    own_copy.wait()
    w_copy.wait()
    step_width = 1024
    slab_width = width // n
    my_columns = pl.ds(pl.multiple_of(me * slab_width, slab_width), slab_width)

    def product(first, count):
        acc[...] = jnp.zeros_like(acc)

        def body(k, carry):
            columns = pl.ds(pl.multiple_of(k * step_width, step_width), step_width)
            block = held[first : first + count, :, columns].reshape(count * rows, step_width)
            acc[: count * rows, :] += lax.dot_general(
                block,
                wbuf[:, columns],
                (((1,), (1,)), ((), ())),
                preferred_element_type=jnp.float32,
            )
            return carry

        lax.fori_loop(0, width // step_width, body, 0)

    def backward(slot, at, origin):
        slab_ref[slot] = held[slot, :, my_columns]
        where = shard_rows(origin)

        def body(head, carry):
            columns = pl.ds(pl.multiple_of(head * HD, HD), HD)
            grad = acc[at * rows : (at + 1) * rows, columns].astype(jnp.bfloat16)
            prob_grad = lax.dot_general(
                grad,
                kv_ref[1],
                (((1,), (1,)), ((), ())),
                preferred_element_type=jnp.float32,
            )
            delta = jnp.sum(
                grad.astype(jnp.float32) * attended[where, columns].astype(jnp.float32),
                axis=1,
                keepdims=True,
            )
            score_grad = (probs[head, where, :].astype(jnp.float32) * (prob_grad - delta)).astype(jnp.bfloat16)
            result = jnp.dot(score_grad, kv_ref[0], preferred_element_type=jnp.float32) * scale
            grad_ref[where, columns] = result.astype(jnp.bfloat16)
            return carry

        lax.fori_loop(0, heads, body, 0)

    def event(hop, turn):
        for direction in range(2):
            part = parts(direction, hop)[turn]
            sent[direction, hop, part].wait_recv()
            if hop < last and part in parts(direction, hop + 1):
                sent[direction, hop + 1, part] = send_part(direction, hop + 1, part)

    event(1, 0)
    advance()
    product(0, 1)
    advance()
    event(1, 1)
    advance()
    backward(0, 0, place)
    for hop in range(1, last + 1):
        turns = 2 if hop < last else 1
        if hop > 1:
            event(hop, 0)
            advance()
            if turns == 2:
                event(hop, 1)
                advance()
        product(slot_of(0, hop, n), turns)
        advance()
        for direction in range(turns):
            backward(slot_of(direction, hop, n), direction, arrival(direction, hop))
    while small:
        advance()
    for copies in (sent, summed, picks):
        for copy in copies.values():
            copy.wait_send()


def ring_block(cotangent, out_weight, queries, kv_local, chooser, n):
    rows, width = cotangent.shape
    outs = out_weight.shape[0]
    tokens = n * rows
    lanes = chooser.shape[1] // 2
    vmem = pl.BlockSpec(memory_space=pltpu.VMEM)
    hbm = pl.BlockSpec(memory_space=pl.ANY)
    dma = pltpu.SemaphoreType.DMA
    return pl.pallas_call(
        functools.partial(block_kernel, n),
        out_shape=(
            jax.ShapeDtypeStruct((tokens, outs), jnp.bfloat16),
            jax.ShapeDtypeStruct((n, rows, width // n), jnp.bfloat16),
            jax.ShapeDtypeStruct((n, rows, 2 * lanes), jnp.bfloat16),
        ),
        in_specs=[hbm, hbm, vmem, vmem, vmem],
        out_specs=(vmem, vmem, vmem),
        scratch_shapes=[
            pltpu.VMEM((n, rows, width), jnp.bfloat16),
            pltpu.VMEM((outs, width), jnp.bfloat16),
            pltpu.VMEM((2 * rows, outs), jnp.float32),
            pltpu.VMEM((outs // HD, tokens, tokens), jnp.bfloat16),
            pltpu.VMEM((tokens, outs), jnp.bfloat16),
            pltpu.VMEM((tokens, 2 * lanes), jnp.bfloat16),
            pltpu.VMEM((2, n - 1, rows, lanes), jnp.bfloat16),
            dma((2, n // 2, 2)),
            dma((2, n // 2, 2)),
            dma((2, n - 1)),
            dma((2, n - 1)),
            dma((2, n // 2)),
            dma((2, n // 2)),
            dma((2,)),
        ],
        compiler_params=pltpu.CompilerParams(
            collective_id=0, has_side_effects=True, vmem_limit_bytes=63 * 1024 * 1024
        ),
    )(cotangent, out_weight, queries, kv_local, chooser)


def owner_kernel(m, part_ref, out_ref, inbox, total, core_send, core_recv, far_send, far_recv):
    chips = m // 2
    me = lax.axis_index("dp")
    chip, core = me // 2, me % 2
    partner = chip * 2 + 1 - core
    barrier = pltpu.get_barrier_semaphore()
    peers = [partner] + [((chip + j) % chips) * 2 + core for j in range(1, chips)]
    for peer in peers:
        pl.semaphore_signal(barrier, inc=1, device_id={"dp": peer}, device_id_type=MESH)
    pl.semaphore_wait(barrier, len(peers))
    pieces = CAP
    rows = out_ref.shape[0] // pieces

    copies = []

    def remote(source, target, send, recv, peer):
        copy = pltpu.make_async_remote_copy(
            src_ref=source, dst_ref=target, send_sem=send, recv_sem=recv,
            device_id={"dp": peer}, device_id_type=MESH,
        )
        copy.start()
        copies.append(copy)
        return copy

    near = {}
    for j in list(range(1, chips)) + [0]:
        for piece in range(pieces):
            at = pl.ds(piece * rows, rows)
            owner = ((chip + j) % chips) * 2 + 1 - core
            near[j, piece] = remote(
                part_ref.at[owner, at], inbox.at[0, j, at],
                core_send.at[j, piece], core_recv.at[j, piece], partner,
            )
    far = {}
    for j in range(1, chips):
        owner = ((chip + j) % chips) * 2 + core
        for piece in range(pieces):
            at = pl.ds(piece * rows, rows)
            near[j, piece].wait_recv()
            both = part_ref[owner, at].astype(jnp.float32) + inbox[0, j, at].astype(jnp.float32)
            total[j - 1, at] = both.astype(jnp.bfloat16)
            far[j, piece] = remote(
                total.at[j - 1, at], inbox.at[1, j, at],
                far_send.at[j, piece], far_recv.at[j, piece], owner,
            )
    for piece in range(pieces):
        at = pl.ds(piece * rows, rows)
        near[0, piece].wait_recv()
        out_ref[at] = part_ref[me, at].astype(jnp.float32) + inbox[0, 0, at].astype(jnp.float32)
    for piece in range(pieces):
        at = pl.ds(piece * rows, rows)
        for j in range(1, chips):
            far[j, piece].wait_recv()
            out_ref[at] += inbox[1, j, at].astype(jnp.float32)
    for copy in copies:
        copy.wait_send()


def sum_at_owners(parts):
    owners, rows, columns = parts.shape
    chips = owners // 2
    dma = pltpu.SemaphoreType.DMA
    vmem = pl.BlockSpec(memory_space=pltpu.VMEM)
    return pl.pallas_call(
        functools.partial(owner_kernel, owners),
        out_shape=jax.ShapeDtypeStruct((rows, columns), jnp.float32),
        in_specs=[vmem],
        out_specs=vmem,
        scratch_shapes=[
            pltpu.VMEM((2, chips, rows, columns), jnp.bfloat16),
            pltpu.VMEM((max(chips - 1, 1), rows, columns), jnp.bfloat16),
            dma((chips, CAP)),
            dma((chips, CAP)),
            dma((chips, CAP)),
            dma((chips, CAP)),
        ],
        compiler_params=pltpu.CompilerParams(
            collective_id=1, has_side_effects=True, vmem_limit_bytes=32 * 1024 * 1024
        ),
    )(parts)


def on_device(queries, keys_values, out_weight, cotangent, head_pick, owner_index):
    tensor_size = lax.axis_size("tensor")
    tensor_rank = lax.axis_index("tensor")
    owners = lax.axis_size("dp")
    local_heads = queries.shape[1] // HD
    kv_head = tensor_rank * local_heads // (H // KVH)
    kv_local = lax.dynamic_slice_in_dim(keys_values, kv_head * HD, HD, 2)

    routing = route_table(owner_index, owners, CAP)
    places = routing.shape[0]
    local_pick = lax.dynamic_slice_in_dim(head_pick, tensor_rank * local_heads, local_heads, 1)
    wanted = jnp.sum(routing[:, :, None] * local_pick.astype(jnp.float32)[None], axis=1)
    spread = jnp.repeat(jnp.repeat(wanted.T, HD, axis=0), HD, axis=1)
    row = lax.broadcasted_iota(jnp.int32, spread.shape, 0) % HD
    column = lax.broadcasted_iota(jnp.int32, spread.shape, 1) % HD
    chooser = jnp.where(row == column, spread, 0.0).astype(jnp.bfloat16)

    query_grad, column_slab, picked = ring_block(
        cotangent, out_weight, queries, kv_local, chooser, tensor_size
    )
    tokens = queries.shape[0]
    selected = lax.dot_general(
        picked.reshape(tokens, places * HD),
        column_slab.reshape(tokens, -1),
        (((0,), (0,)), ((), ())),
        preferred_element_type=jnp.float32,
    ).astype(jnp.bfloat16)
    owned = sum_at_owners(selected.reshape(owners, CAP * HD, -1))
    return (query_grad, owned.reshape(CAP, HD, -1))


def solution(mesh):
    placed = (
        P("dp", "tensor"),
        P(None, "dp", None),
        P("tensor", None),
        P(("dp", "tensor"), None),
        P(),
        P(),
    )
    return jax.shard_map(
        on_device,
        mesh=mesh,
        in_specs=placed,
        out_specs=(P("dp", "tensor"), P("dp", None, "tensor")),
        check_vma=False,
    )
```

```python
import functools
import math

import jax
import jax.numpy as jnp
from jax import lax
from jax.experimental import pallas as pl
from jax.experimental.pallas import tpu as pltpu
from jax.sharding import PartitionSpec as P

H = 64
HD = 128
KVH = 8
CAP = 3
HD_BITS = 7
PARTS = 4
WINDOW = 2
UNROLL = 4
MESH = pl.DeviceIdType.MESH


def ring_member(place, n):
    late = place // (n // 2)
    return (1 - late) * (2 * place) + late * (2 * (n - 1 - place) + 1)


def ring_place(index, n):
    odd = index % 2
    return (1 - odd) * (index // 2) + odd * (n - 1 - index // 2)


def slot_of(direction, hop, n):
    if hop == 0:
        return 0
    if hop == n // 2:
        return n - 1
    return 2 * hop - 1 + direction


def block_kernel(
    n, cot_ref, w_ref, all_kv_ref, q_ref, pick_ref, owner_ref, owner_row_ref,
    grad_ref, slab_ref, picked_ref,
    held, wbuf, kv_ref, chooser_ref, acc, probs, attended, mine, sums,
    send_sem, recv_sem, sum_send, sum_recv, pick_send, pick_recv, local_sem,
):
    rows, width = cot_ref.shape
    piece = width // PARTS
    last = n // 2
    tokens = n * rows
    heads = q_ref.shape[1] // HD
    lanes = mine.shape[1] // 2
    scale = 1.0 / math.sqrt(HD)
    me = lax.axis_index("tensor")
    place = ring_place(me, n)
    to = (ring_member((place + 1) % n, n), ring_member((place + n - 1) % n, n))

    w_copy = pltpu.make_async_copy(w_ref, wbuf, local_sem.at[0])
    w_copy.start()
    own_copy = pltpu.make_async_copy(cot_ref, held.at[0], local_sem.at[1])
    own_copy.start()
    kv_head = me * heads // (H // KVH)
    kv_copy = pltpu.make_async_copy(
        all_kv_ref.at[:, :, pl.ds(pl.multiple_of(kv_head * HD, HD), HD)], kv_ref, local_sem.at[2]
    )
    kv_copy.start()

    barrier = pltpu.get_barrier_semaphore()
    for target in to:
        pl.semaphore_signal(barrier, inc=1, device_id={"tensor": target}, device_id_type=MESH)
    pl.semaphore_wait(barrier, 2)

    def remote(source, target, send, recv, direction):
        copy = pltpu.make_async_remote_copy(
            src_ref=source,
            dst_ref=target,
            send_sem=send,
            recv_sem=recv,
            device_id={"tensor": to[direction]},
            device_id_type=MESH,
        )
        copy.start()
        return copy

    def send_part(direction, hop, part):
        columns = pl.ds(part * piece, piece)
        source = cot_ref if hop == 1 else held.at[slot_of(direction, hop - 1, n)]
        return remote(
            source.at[:, columns],
            held.at[slot_of(direction, hop, n), :, columns],
            send_sem.at[direction, hop - 1, part],
            recv_sem.at[direction, hop - 1, part],
            direction,
        )

    def shard_rows(at):
        return pl.ds(pl.multiple_of(ring_member(at, n) * rows, rows), rows)

    def arrival(direction, hop):
        return (place + (n - hop if direction == 0 else hop)) % n

    def side(direction):
        return pl.ds(direction * lanes, lanes)

    def send_sum(direction, step):
        if step == 1:
            source = mine.at[shard_rows(arrival(direction, 1)), side(direction)]
        else:
            source = sums.at[direction, step - 2]
        return remote(
            source,
            sums.at[direction, step - 1],
            sum_send.at[direction, step - 1],
            sum_recv.at[direction, step - 1],
            direction,
        )

    def send_pick(direction, hop):
        columns = pl.ds(0, 2 * lanes) if hop < last else side(direction)
        return remote(
            picked_ref.at[slot_of(direction, hop - 1, n), :, columns],
            picked_ref.at[slot_of(direction, hop, n), :, columns],
            pick_send.at[direction, hop - 1],
            pick_recv.at[direction, hop - 1],
            direction,
        )

    sent, summed, picks = {}, {}, {}

    def sum_step(step):
        for direction in range(2):
            summed[direction, step].wait_recv()
            term = mine[shard_rows(arrival(direction, step + 1)), side(direction)]
            total = sums[direction, step - 1].astype(jnp.float32) + term.astype(jnp.float32)
            if step < n - 1:
                sums[direction, step - 1] = total.astype(jnp.bfloat16)
                summed[direction, step + 1] = send_sum(direction, step + 1)
            else:
                picked_ref[0, :, side(direction)] = total.astype(jnp.bfloat16)
        if step == n - 1:
            for direction in range(2):
                picks[direction, 1] = send_pick(direction, 1)

    def pick_step(hop):
        for direction in range(2):
            picks[direction, hop].wait_recv()
            if hop < last:
                picks[direction, hop + 1] = send_pick(direction, hop + 1)

    small = [functools.partial(sum_step, step) for step in range(1, n)]
    small += [functools.partial(pick_step, hop) for hop in range(1, last + 1)]

    def advance():
        if small:
            small.pop(0)()

    turns = [(hop, turn) for hop in range(1, last) for turn in range(PARTS)]
    turns += [(last, turn) for turn in range(PARTS // 2)]

    def part_at(direction, turn):
        return turn if direction == 0 else PARTS - 1 - turn

    def send_turn(number):
        hop, turn = turns[number]
        for direction in range(2):
            part = part_at(direction, turn)
            sent[direction, hop, part] = send_part(direction, hop, part)

    ahead = min(PARTS, len(turns))
    for number in range(ahead):
        send_turn(number)

    count = owner_ref.shape[0]
    chosen = owner_ref[...]
    order = lax.broadcasted_iota(jnp.int32, (count, count), 0)
    other = lax.broadcasted_iota(jnp.int32, (count, count), 1)
    alike = (chosen == owner_row_ref[...]) & (order > other)
    slot_index = jnp.sum(jnp.where(alike, 1.0, 0.0), axis=1, keepdims=True)
    goal = chosen.astype(jnp.float32) * CAP + slot_index
    place_at = lax.broadcasted_iota(jnp.int32, (count, 2 * lanes), 1) >> HD_BITS
    routed = jnp.where(goal == place_at.astype(jnp.float32), 1.0, 0.0)
    head_at = lax.broadcasted_iota(jnp.int32, (q_ref.shape[1], H), 0) >> HD_BITS
    head_of = lax.broadcasted_iota(jnp.int32, (q_ref.shape[1], H), 1)
    local = jnp.where(head_at + me * heads == head_of, 1.0, 0.0)
    named = lax.dot_general(
        local,
        pick_ref[...].astype(jnp.float32),
        (((1,), (1,)), ((), ())),
        preferred_element_type=jnp.float32,
    )
    spread = jnp.dot(named, routed, preferred_element_type=jnp.float32)
    row = lax.broadcasted_iota(jnp.int32, spread.shape, 0) & (HD - 1)
    column = lax.broadcasted_iota(jnp.int32, spread.shape, 1) & (HD - 1)
    chooser_ref[...] = jnp.where(row == column, spread, 0.0).astype(jnp.bfloat16)
    kv_copy.wait()

    tile = 128

    def forward(head, carry):
        columns = pl.ds(pl.multiple_of(head * HD, HD), HD)
        for base in range(0, tokens, tile):
            span = base + tile
            score = (
                lax.dot_general(
                    q_ref[base:span, columns],
                    kv_ref[0, :span, :],
                    (((1,), (1,)), ((), ())),
                    preferred_element_type=jnp.float32,
                )
                * scale
            )
            at = lax.broadcasted_iota(jnp.int32, (tile, span), 0) + base
            key_at = lax.broadcasted_iota(jnp.int32, (tile, span), 1)
            score = jnp.where(at >= key_at, score, -jnp.inf)
            weight = jnp.exp(score - jnp.max(score, axis=1, keepdims=True))
            prob = (weight / jnp.sum(weight, axis=1, keepdims=True)).astype(jnp.bfloat16)
            probs[head, base:span, :span] = prob
            if span < tokens:
                probs[head, base:span, span:] = jnp.zeros((tile, tokens - span), jnp.bfloat16)
            attended[base:span, columns] = jnp.dot(
                prob, kv_ref[1, :span, :], preferred_element_type=jnp.float32
            ).astype(jnp.bfloat16)
        return carry

    lax.fori_loop(0, heads, forward, 0)

    def choose(block, carry):
        at = pl.ds(pl.multiple_of(block * tile, tile), tile)
        mine[at, :] = jnp.dot(
            attended[at, :], chooser_ref[...], preferred_element_type=jnp.float32
        ).astype(jnp.bfloat16)
        return carry

    lax.fori_loop(0, tokens // tile, choose, 0)
    for direction in range(2):
        summed[direction, 1] = send_sum(direction, 1)

    own_copy.wait()
    w_copy.wait()
    step_width = 1024
    slab_width = width // n
    my_columns = pl.ds(pl.multiple_of(me * slab_width, slab_width), slab_width)

    def product(first, count, begin, end):
        if begin == 0:
            acc[...] = jnp.zeros_like(acc)

        def body(k, carry):
            columns = pl.ds(pl.multiple_of(k * step_width, step_width), step_width)
            block = held[first : first + count, :, columns].reshape(count * rows, step_width)
            acc[: count * rows, :] += lax.dot_general(
                block,
                wbuf[:, columns],
                (((1,), (1,)), ((), ())),
                preferred_element_type=jnp.float32,
            )
            return carry

        steps = width // step_width
        lax.fori_loop(begin * steps // 2, end * steps // 2, body, 0)

    def backward(slot, at, origin):
        slab_ref[slot] = held[slot, :, my_columns]
        where = shard_rows(origin)

        def body(head, carry):
            columns = pl.ds(pl.multiple_of(head * HD, HD), HD)
            grad = acc[at * rows : (at + 1) * rows, columns].astype(jnp.bfloat16)
            prob_grad = lax.dot_general(
                grad,
                kv_ref[1],
                (((1,), (1,)), ((), ())),
                preferred_element_type=jnp.float32,
            )
            delta = jnp.sum(
                grad.astype(jnp.float32) * attended[where, columns].astype(jnp.float32),
                axis=1,
                keepdims=True,
            )
            score_grad = (probs[head, where, :].astype(jnp.float32) * (prob_grad - delta)).astype(jnp.bfloat16)
            result = jnp.dot(score_grad, kv_ref[0], preferred_element_type=jnp.float32) * scale
            grad_ref[where, columns] = result.astype(jnp.bfloat16)
            return carry

        lax.fori_loop(0, heads, body, 0, unroll=UNROLL)

    work = []

    def queue(first, origins):
        count = len(origins)
        work.append(functools.partial(product, first, count, 0, 1))
        work.append(functools.partial(product, first, count, 1, 2))
        for at, origin in enumerate(origins):
            work.append(functools.partial(backward, first + at, at, origin))

    queue(0, [place])
    for number, (hop, turn) in enumerate(turns):
        for direction in range(2):
            sent[direction, hop, part_at(direction, turn)].wait_recv()
        if ahead <= number + WINDOW < len(turns):
            send_turn(number + WINDOW)
        advance()
        if number + 1 == len(turns):
            queue(n - 1, [arrival(0, last)])
        elif turns[number + 1][0] != hop:
            queue(slot_of(0, hop, n), [arrival(0, hop), arrival(1, hop)])
        if work:
            work.pop(0)()
    while small or work:
        advance()
        if work:
            work.pop(0)()
    for copies in (sent, summed, picks):
        for copy in copies.values():
            copy.wait_send()


def ring_block(cotangent, out_weight, keys_values, queries, head_pick, owner_index, places, n):
    rows, width = cotangent.shape
    outs = out_weight.shape[0]
    tokens = n * rows
    lanes = places * HD // 2
    vmem = pl.BlockSpec(memory_space=pltpu.VMEM)
    hbm = pl.BlockSpec(memory_space=pl.ANY)
    dma = pltpu.SemaphoreType.DMA
    return pl.pallas_call(
        functools.partial(block_kernel, n),
        out_shape=(
            jax.ShapeDtypeStruct((tokens, outs), jnp.bfloat16),
            jax.ShapeDtypeStruct((n, rows, width // n), jnp.bfloat16),
            jax.ShapeDtypeStruct((n, rows, 2 * lanes), jnp.bfloat16),
        ),
        in_specs=[hbm, hbm, hbm, vmem, vmem, vmem, vmem],
        out_specs=(vmem, vmem, vmem),
        scratch_shapes=[
            pltpu.VMEM((n, rows, width), jnp.bfloat16),
            pltpu.VMEM((outs, width), jnp.bfloat16),
            pltpu.VMEM((2, tokens, HD), jnp.bfloat16),
            pltpu.VMEM((outs, 2 * lanes), jnp.bfloat16),
            pltpu.VMEM((2 * rows, outs), jnp.float32),
            pltpu.VMEM((outs // HD, tokens, tokens), jnp.bfloat16),
            pltpu.VMEM((tokens, outs), jnp.bfloat16),
            pltpu.VMEM((tokens, 2 * lanes), jnp.bfloat16),
            pltpu.VMEM((2, n - 1, rows, lanes), jnp.bfloat16),
            dma((2, n // 2, PARTS)),
            dma((2, n // 2, PARTS)),
            dma((2, n - 1)),
            dma((2, n - 1)),
            dma((2, n // 2)),
            dma((2, n // 2)),
            dma((3,)),
        ],
        compiler_params=pltpu.CompilerParams(
            collective_id=0, has_side_effects=True, vmem_limit_bytes=63 * 1024 * 1024
        ),
    )(
        cotangent, out_weight, keys_values, queries,
        head_pick, owner_index, owner_index.reshape(1, -1),
    )


def owner_kernel(m, part_ref, out_ref, inbox, total, core_send, core_recv, far_send, far_recv):
    chips = m // 2
    me = lax.axis_index("dp")
    chip, core = me // 2, me % 2
    partner = chip * 2 + 1 - core
    barrier = pltpu.get_barrier_semaphore()
    peers = [partner] + [((chip + j) % chips) * 2 + core for j in range(1, chips)]
    for peer in peers:
        pl.semaphore_signal(barrier, inc=1, device_id={"dp": peer}, device_id_type=MESH)
    pl.semaphore_wait(barrier, len(peers))
    pieces = CAP
    rows = out_ref.shape[0] // pieces

    copies = []

    def remote(source, target, send, recv, peer):
        copy = pltpu.make_async_remote_copy(
            src_ref=source, dst_ref=target, send_sem=send, recv_sem=recv,
            device_id={"dp": peer}, device_id_type=MESH,
        )
        copy.start()
        copies.append(copy)
        return copy

    near = {}
    for j in list(range(1, chips)) + [0]:
        for piece in range(pieces):
            at = pl.ds(piece * rows, rows)
            owner = ((chip + j) % chips) * 2 + 1 - core
            near[j, piece] = remote(
                part_ref.at[owner, at], inbox.at[0, j, at],
                core_send.at[j, piece], core_recv.at[j, piece], partner,
            )
    far = {}
    for j in range(1, chips):
        owner = ((chip + j) % chips) * 2 + core
        for piece in range(pieces):
            at = pl.ds(piece * rows, rows)
            near[j, piece].wait_recv()
            both = part_ref[owner, at].astype(jnp.float32) + inbox[0, j, at].astype(jnp.float32)
            total[j - 1, at] = both.astype(jnp.bfloat16)
            far[j, piece] = remote(
                total.at[j - 1, at], inbox.at[1, j, at],
                far_send.at[j, piece], far_recv.at[j, piece], owner,
            )
    for piece in range(pieces):
        at = pl.ds(piece * rows, rows)
        near[0, piece].wait_recv()
        out_ref[at] = part_ref[me, at].astype(jnp.float32) + inbox[0, 0, at].astype(jnp.float32)
    for piece in range(pieces):
        at = pl.ds(piece * rows, rows)
        for j in range(1, chips):
            far[j, piece].wait_recv()
            out_ref[at] += inbox[1, j, at].astype(jnp.float32)
    for copy in copies:
        copy.wait_send()


def sum_at_owners(parts):
    owners, rows, columns = parts.shape
    chips = owners // 2
    dma = pltpu.SemaphoreType.DMA
    vmem = pl.BlockSpec(memory_space=pltpu.VMEM)
    return pl.pallas_call(
        functools.partial(owner_kernel, owners),
        out_shape=jax.ShapeDtypeStruct((rows, columns), jnp.float32),
        in_specs=[vmem],
        out_specs=vmem,
        scratch_shapes=[
            pltpu.VMEM((2, chips, rows, columns), jnp.bfloat16),
            pltpu.VMEM((max(chips - 1, 1), rows, columns), jnp.bfloat16),
            dma((chips, CAP)),
            dma((chips, CAP)),
            dma((chips, CAP)),
            dma((chips, CAP)),
        ],
        compiler_params=pltpu.CompilerParams(
            collective_id=1, has_side_effects=True, vmem_limit_bytes=32 * 1024 * 1024
        ),
    )(parts)


def on_device(queries, keys_values, out_weight, cotangent, head_pick, owner_index):
    tensor_size = lax.axis_size("tensor")
    owners = lax.axis_size("dp")
    places = owners * CAP
    query_grad, column_slab, picked = ring_block(
        cotangent, out_weight, keys_values, queries, head_pick, owner_index, places, tensor_size
    )
    tokens = queries.shape[0]
    selected = lax.dot_general(
        picked.reshape(tokens, places * HD),
        column_slab.reshape(tokens, -1),
        (((0,), (0,)), ((), ())),
        preferred_element_type=jnp.float32,
    ).astype(jnp.bfloat16)
    owned = sum_at_owners(selected.reshape(owners, CAP * HD, -1))
    return (query_grad, owned.reshape(CAP, HD, -1))


def solution(mesh):
    placed = (
        P("dp", "tensor"),
        P(None, "dp", None),
        P("tensor", None),
        P(("dp", "tensor"), None),
        P(),
        P(),
    )
    return jax.shard_map(
        on_device,
        mesh=mesh,
        in_specs=placed,
        out_specs=(P("dp", "tensor"), P("dp", None, "tensor")),
        check_vma=False,
    )
```
